32 devices in a mesh: island: 4 (over z), fsdp: 2 (over x), tensor: 4 (over y, core).
Axes of the slice: x: 2, y: 2, z: 4, core: 2. Of those that a mesh axis runs over, the one named last changes fastest.
Arguments:
- hidden: bfloat16 [4, 256, 14336], P('island', 'fsdp', 'tensor'), may hold values from -6 to 6
- target: bfloat16 [4, 256, 4096], P('island', 'tensor', 'fsdp'), may hold values from -6 to 6
- valid: int32 [4, 256], P('island', 'fsdp'), may hold values from 0 to 1, as said below
- island_tokens: int32 [4], replicated, may hold values from 4096 to 16384
- inner_weight: bfloat16 [4, 14336, 4096], P('island', 'tensor', 'fsdp'), may hold values from -6 to 6
- adam_first: bfloat16 [4, 14336, 4096], P('island', 'tensor', 'fsdp'), may hold values from -0.0014648438 to 0.0014648438
- adam_second: bfloat16 [4, 14336, 4096], P('island', 'tensor', 'fsdp'), may hold values from 6.798655e-08 to 1.0877848e-06
- anchor: bfloat16 [14336, 4096], P('tensor', 'fsdp'), may hold values from -6 to 6
- outer_momentum: bfloat16 [14336, 4096], P('tensor', 'fsdp'), may hold values from -6 to 6
Outputs:
- new_weight: bfloat16 [14336, 4096], P('tensor', 'fsdp')
- new_momentum: bfloat16 [14336, 4096], P('tensor', 'fsdp')
The draws below stay inside these ranges and needn't reach their ends.
Inputs may be any that keep to these rules, and one draw needn't show every extreme that they name: The first token of each block of 128 tokens is valid.
All inputs are finite; a program needn't handle non-finite values.
Results may differ from the reference program's by a relative error of at most 0.003.
Values may be sent and summed in bfloat16 or wider, within the bound.
No kernel may reach another device: no remote copies, remote signals or barrier semaphores. Data moves between devices by JAX's collectives and lax.ppermute only.
A program may use at most 320 MiB of HBM per device.

```python
import math
import jax
import jax.numpy as jnp
from jax import lax

DW = 4096
FFW = 14336
TOK_DEV = 128
ISLANDS = 4
TOKENS = 256


def draw_valid(key, part):
    ticket = jax.random.randint(key, (ISLANDS, TOKENS), 0, 1000)
    position = jnp.arange(TOKENS, dtype=jnp.int32)
    device = position // TOK_DEV
    blocks = TOKENS // TOK_DEV
    cutoff = 250 + 500 * device // max(blocks - 1, 1)
    leading = position % TOK_DEV == 0
    chosen = jnp.logical_or(ticket < cutoff[None, :], leading[None, :])
    return chosen.astype(jnp.int32)


def touch_ends(drawn, own_key, least, high):
    extent = drawn.shape
    index_at = [jax.random.randint(jax.random.fold_in(own_key, axis), (), 0, extent[axis]) for axis in range(len(extent))]
    drawn = drawn.at[tuple(index_at)].set(least)
    longest = extent.index(max(extent))
    index_at[longest] = (index_at[longest] + 1) % extent[longest]
    return drawn.at[tuple(index_at)].set(high)


def block_scale(rng, shape, shards, smallest, high):
    gain = 1.0
    for dim, blocks in shards:
        draws = jax.random.uniform(jax.random.fold_in(jax.random.fold_in(rng, 6), dim), (blocks,), jnp.float32, smallest / len(shards), high / len(shards))
        gain = gain * jnp.repeat(jnp.exp(draws), shape[dim] // blocks).reshape((-1,) + (1,) * (len(shape) - 1 - dim))
    return gain


def normal_values(stream_key, dims, width, reach, pieces=(), kind=jnp.bfloat16):
    loudness = block_scale(stream_key, dims, pieces, -0.22, 0.18) if pieces else 1.0
    entries = jax.random.normal(stream_key, dims, jnp.float32) * width * loudness
    return jnp.minimum(jnp.maximum(entries, -reach), reach).astype(kind)


def setup_inputs(seed: int = 0) -> dict:
    streams_of = jax.random.split(jax.random.key(seed), 10)
    hidden = normal_values(streams_of[0], (ISLANDS, TOKENS, FFW), 1.0, 6.0, ((0, 4), (1, 2), (2, 4)))
    target = normal_values(streams_of[1], (ISLANDS, TOKENS, DW), 1.0, 6.0, ((0, 4), (1, 4), (2, 2)))
    valid = draw_valid(jax.random.fold_in(streams_of[9], 71), 0)
    island_tokens = touch_ends(jax.random.randint(streams_of[3], (ISLANDS,), 4096, 16385), jax.random.fold_in(streams_of[3], 1), 4096, 16384).astype(jnp.int32)
    inner_weight = normal_values(streams_of[4], (ISLANDS, FFW, DW), 1.0, 6.0, ((0, 4), (1, 4), (2, 2)))
    adam_first = normal_values(streams_of[5], (ISLANDS, FFW, DW), (0.2 * (FFW * TOKENS) ** -0.5), 0.0014648438, ((0, 4), (1, 4), (2, 2)))
    adam_second = jnp.clip(jnp.exp(math.log(1.087784767150879e-06) - 2.7725887 * jax.random.uniform(streams_of[6], (ISLANDS, FFW, DW), jnp.float32) ** block_scale(streams_of[6], (ISLANDS, FFW, DW), ((0, 4), (1, 4), (2, 2)), -0.2, 0.2)), 6.798654794692993e-08, 1.087784767150879e-06).astype(jnp.bfloat16)
    anchor = normal_values(streams_of[7], (FFW, DW), 1.0, 6.0, ((0, 4), (1, 2)))
    outer_momentum = normal_values(streams_of[8], (FFW, DW), 0.5, 6.0, ((0, 4), (1, 2)))
    return {"hidden": hidden, "target": target, "valid": valid, "island_tokens": island_tokens, "inner_weight": inner_weight, "adam_first": adam_first, "adam_second": adam_second, "anchor": anchor, "outer_momentum": outer_momentum}


beta_first = 0.9
beta_second = 0.95
epsilon = 1e-08
inner_rate = 0.5
decay_rate = 0.1
outer_rate = 0.7
nesterov_mu = 0.9

def reference(hidden, target, valid, island_tokens, inner_weight, adam_first, adam_second, anchor, outer_momentum):
    factor = FFW ** (-0.5)
    totals = island_tokens.astype(jnp.float32)
    portions = totals / jnp.sum(totals)
    anchor_wide = anchor.astype(jnp.float32)
    average_step = jnp.zeros(anchor.shape, jnp.float32)
    for island in range(ISLANDS):
        keep_mask = valid[island].astype(jnp.bfloat16)
        masked = hidden[island] * keep_mask[:, None]
        tallies = jnp.sum(valid[island].astype(jnp.float32))
        output = factor * jnp.dot(masked, inner_weight[island], preferred_element_type=jnp.float32)
        cotangent = ((output - target[island].astype(jnp.float32)) / tallies).astype(jnp.bfloat16)
        gradient = factor * lax.dot_general(masked, cotangent, (((0,), (0,)), ((), ())), preferred_element_type=jnp.float32)
        weights = inner_weight[island].astype(jnp.float32)
        first = beta_first * adam_first[island].astype(jnp.float32) + (1.0 - beta_first) * gradient
        second = beta_second * adam_second[island].astype(jnp.float32) + (1.0 - beta_second) * gradient * gradient
        inner_new = weights - inner_rate * (first / (jnp.sqrt(second) + epsilon) + decay_rate * weights)
        average_step = average_step + portions[island] * (anchor_wide - inner_new)
    momentum = nesterov_mu * outer_momentum.astype(jnp.float32) + average_step
    new_weight = (anchor_wide - outer_rate * (average_step + nesterov_mu * momentum)).astype(jnp.bfloat16)
    return (new_weight, momentum.astype(jnp.bfloat16))
```

```python
import functools

import jax
import jax.numpy as jnp
from jax import lax
from jax.sharding import PartitionSpec as P

FFW = 14336

beta_first = 0.9
beta_second = 0.95
epsilon = 1e-08
inner_rate = 0.5
decay_rate = 0.1
outer_rate = 0.7
nesterov_mu = 0.9

F32, F16, BF16 = jnp.float32, jnp.float16, jnp.bfloat16
WIRE = 4096.0
PIECE = 128
LAG = 2
ENDS = [(0, 1), (1, 0), (2, 3), (3, 2)]
MIDDLE = [(1, 2), (2, 1)]

fence = lax.optimization_barrier


def gather_tokens(own, valid_own, weight, fsdp, scale):
    def share(tokens):
        return (jnp.dot(tokens, weight, preferred_element_type=F32) * scale).astype(F16)

    if fsdp == 2:
        swap = [(0, 1), (1, 0)]
        other = lax.ppermute(own, "fsdp", swap)
        valid_other = lax.ppermute(valid_own, "fsdp", swap)
        leading = lax.axis_index("fsdp") == 0

        def in_order(a, b):
            return jnp.concatenate([jnp.where(leading, a, b), jnp.where(leading, b, a)], axis=0)

        partial = in_order(share(own), share(other))
        return in_order(own, other), in_order(valid_own, valid_other), partial
    tokens = lax.all_gather(own, "fsdp", axis=0, tiled=True)
    return tokens, lax.all_gather(valid_own, "fsdp", axis=0, tiled=True), share(tokens)


def cotangent_of(partial, target, valid_all, tensor, scale, factor):
    me = lax.axis_index("tensor")
    block = target.shape[0]

    def mine(array, owner):
        return lax.dynamic_slice_in_dim(array, owner * block, block, axis=0)

    total = mine(partial, me).astype(F32)
    for step in range(1, tensor):
        ring = [(i, (i + step) % tensor) for i in range(tensor)]
        total += lax.ppermute(mine(partial, (me + step) % tensor), "tensor", ring).astype(F32)
    keep = mine(valid_all, me)[:, None]
    output = keep * total * (factor / scale)
    tallies = jnp.sum(valid_all)
    cot = (keep * ((output - target.astype(F32)) / tallies)).astype(BF16)
    whole = jnp.zeros((block * tensor, target.shape[1]), BF16)
    whole = lax.dynamic_update_slice_in_dim(whole, cot, me * block, axis=0)
    for step in range(1, tensor):
        ring = [(i, (i + step) % tensor) for i in range(tensor)]
        got = lax.ppermute(cot, "tensor", ring)
        whole = lax.dynamic_update_slice_in_dim(whole, got, ((me - step) % tensor) * block, axis=0)
    return whole


def on_device(fsdp, tensor, hidden, target, valid, island_tokens, inner_weight, adam_first, adam_second, anchor, outer_momentum):
    factor = FFW ** (-0.5)
    rows, cols = inner_weight.shape[1:]
    scale = 32.0
    tokens, valid_all, partial = gather_tokens(hidden[0], valid[0].astype(F32), inner_weight[0], fsdp, scale)
    cot = cotangent_of(partial, target[0], valid_all, tensor, scale, factor)

    island = lax.axis_index("island")
    at_end = (island == 0) | (island == 3)
    totals = island_tokens.astype(F32)
    portion = totals[island] / jnp.sum(totals)

    count = rows // PIECE

    def own_term(k, cot):
        here = slice(k * PIECE, (k + 1) * PIECE)
        gradient = factor * lax.dot_general(
            tokens[:, here], cot, (((0,), (0,)), ((), ())), preferred_element_type=F32
        )
        weights = inner_weight[0, here].astype(F32)
        first = beta_first * adam_first[0, here].astype(F32) + (1.0 - beta_first) * gradient
        second = beta_second * adam_second[0, here].astype(F32) + (1.0 - beta_second) * gradient * gradient
        inner_new = weights - inner_rate * (first / (jnp.sqrt(second) + epsilon) + decay_rate * weights)
        return ((WIRE * portion) * inner_new).astype(F16)

    def plus(a, b):
        return (a.astype(F32) + b.astype(F32)).astype(F16)

    new_weight = jnp.zeros((rows, cols), BF16)
    new_momentum = jnp.zeros((rows, cols), BF16)
    own, sent_end, sent_mid, got_end, got_mid = {}, {}, {}, {}, {}
    for event in range(count + 3 * LAG):
        held = {}
        if event - LAG in got_end:
            held["got_end"] = got_end.pop(event - LAG)
            held["sent_end"] = sent_end.pop(event - LAG)
        if event - LAG in got_mid:
            held["got_mid"] = got_mid.pop(event - LAG)
            held["sent_mid"] = sent_mid.pop(event - LAG)
        if event < count and held:
            held["cot"] = cot
        before = {}
        if event - 1 in sent_end:
            before["end"] = sent_end[event - 1]
        if event - 1 in sent_mid:
            before["mid"] = sent_mid[event - 1]
        if held:
            held, before = fence((held, before))
            cot = held.get("cot", cot)
            if "end" in before:
                sent_end[event - 1] = before["end"]
            if "mid" in before:
                sent_mid[event - 1] = before["mid"]
        summed = None
        if event - LAG in range(LAG, count + LAG):
            summed = plus(held["sent_mid"], held["got_mid"])
        if event < count:
            own[event] = own_term(event, cot)
            sent_end[event] = own[event] if summed is None else jnp.where(at_end, own[event], summed)
        elif summed is not None:
            sent_end[event] = summed
        if event in sent_end:
            got_end[event] = lax.ppermute(sent_end[event], "island", ENDS)
        if event - LAG in own:
            sent_mid[event] = plus(own.pop(event - LAG), held["got_end"])
            got_mid[event] = lax.ppermute(sent_mid[event], "island", MIDDLE)
        k = event - 3 * LAG
        if k >= 0:
            here = slice(k * PIECE, (k + 1) * PIECE)
            mean = jnp.where(at_end, held["got_end"], held["sent_end"]).astype(F32) * (1.0 / WIRE)
            anchor_part = anchor[here].astype(F32)
            average_step = anchor_part - mean
            momentum = nesterov_mu * outer_momentum[here].astype(F32) + average_step
            updated = anchor_part - outer_rate * (average_step + nesterov_mu * momentum)
            new_weight = lax.dynamic_update_slice(new_weight, updated.astype(BF16), (k * PIECE, 0))
            new_momentum = lax.dynamic_update_slice(new_momentum, momentum.astype(BF16), (k * PIECE, 0))
    return new_weight, new_momentum


def solution(mesh):
    return jax.shard_map(
        functools.partial(on_device, mesh.shape["fsdp"], mesh.shape["tensor"]),
        mesh=mesh,
        in_specs=(
            P("island", "fsdp", "tensor"),
            P("island", "tensor", "fsdp"),
            P("island", "fsdp"),
            P(),
            P("island", "tensor", "fsdp"),
            P("island", "tensor", "fsdp"),
            P("island", "tensor", "fsdp"),
            P("tensor", "fsdp"),
            P("tensor", "fsdp"),
        ),
        out_specs=(P("tensor", "fsdp"), P("tensor", "fsdp")),
        check_vma=False,
    )
```

```python
import functools

import jax
import jax.numpy as jnp
from jax import lax
from jax.experimental import pallas as pl
from jax.experimental.pallas import tpu as pltpu
from jax.sharding import PartitionSpec as P

FFW = 14336
factor = FFW ** (-0.5)

beta_first = 0.9
beta_second = 0.95
epsilon = 1e-08
inner_rate = 0.5
decay_rate = 0.1
outer_rate = 0.7
nesterov_mu = 0.9

F32, F16, BF16 = jnp.float32, jnp.float16, jnp.bfloat16
WIRE = 4096.0
SHARE = 32.0
QUARTERS = 4
ROW_BLOCKS = 7
PASS = 32
KERNEL_VMEM = 16 * 2**20
LAG = 2
ENDS = [(0, 1), (1, 0), (2, 3), (3, 2)]
MIDDLE = [(1, 2), (2, 1)]

fence = lax.optimization_barrier


def piece_kernel(own_at, outer_at, *refs):
    refs = list(refs)
    sems, written = refs.pop(), refs.pop()
    loaded = refs.pop()
    sources, targets = [], []
    if own_at is not None:
        portion, tokens, cot = refs[:3]
        sources += [ref.at[0, pl.ds(own_at[0], loaded.shape[1]), pl.ds(own_at[1], loaded.shape[2])] for ref in refs[3:6]]
        refs = refs[6:]
    if outer_at is not None:
        mean = refs[0]
        there = (pl.ds(outer_at[0], loaded.shape[1]), pl.ds(outer_at[1], loaded.shape[2]))
        sources = [ref.at[there] for ref in refs[1:3]] + sources
        targets = [ref.at[there] for ref in refs[-2:]]
        refs = refs[3:-2]
    if own_at is not None:
        out = refs[-1]
    loads = [pltpu.make_async_copy(source, loaded.at[n], sems.at[n]) for n, source in enumerate(sources)]
    stores = [pltpu.make_async_copy(written.at[n], target, sems.at[5 + n]) for n, target in enumerate(targets)]
    for load in loads:
        load.start()
    if own_at is not None:
        out[...] = lax.dot_general(
            tokens[:, pl.ds(own_at[0], out.shape[0])],
            cot[:, pl.ds(own_at[2], out.shape[1])],
            (((0,), (0,)), ((), ())),
            preferred_element_type=F32,
        )
    if outer_at is not None:
        loads.pop(0).wait()
        loads.pop(0).wait()

        def finish(i, carry):
            here = pl.ds(pl.multiple_of(i * PASS, PASS), PASS)
            start = loaded[0, here].astype(F32)
            average_step = start - mean[here]
            momentum = nesterov_mu * loaded[1, here].astype(F32) + average_step
            updated = start - outer_rate * (average_step + nesterov_mu * momentum)
            written[0, here] = updated.astype(BF16)
            written[1, here] = momentum.astype(BF16)
            return carry

        lax.fori_loop(0, mean.shape[0] // PASS, finish, 0)
        for store in stores:
            store.start()
    if own_at is not None:
        base = 2 if outer_at is not None else 0
        for load in loads:
            load.wait()
        keep = (WIRE * (1.0 - inner_rate * decay_rate)) * portion[0]
        move = (WIRE * inner_rate) * portion[0]

        def some(i, carry):
            here = pl.ds(pl.multiple_of(i * PASS, PASS), PASS)
            product = out[here]
            first = beta_first * loaded[base + 1, here].astype(F32) + ((1.0 - beta_first) * factor) * product
            second = beta_second * loaded[base + 2, here].astype(F32) + ((1.0 - beta_second) * factor**2) * (
                product * product
            )
            step = first * pl.reciprocal(second * lax.rsqrt(second) + epsilon)
            out[here] = keep * loaded[base, here].astype(F32) - move * step
            return carry

        lax.fori_loop(0, out.shape[0] // PASS, some, 0)
    for store in stores:
        store.wait()


def work(shape, own=None, outer=None):
    height, width = shape
    hbm, vmem = pl.BlockSpec(memory_space=pltpu.HBM), pl.BlockSpec(memory_space=pltpu.VMEM)
    operands, specs, outs, out_specs, aliases, moved, flops = [], [], [], [], {}, 0, 0
    def stay(arrays):
        return [pltpu.with_memory_space_constraint(array, pltpu.HBM) for array in arrays]

    if own:
        operands += [*own[1][:3], *stay(own[1][3:])]
        specs += [pl.BlockSpec(memory_space=pltpu.SMEM), vmem, vmem, hbm, hbm, hbm]
        outs.append(jax.ShapeDtypeStruct(shape, F32))
        out_specs.append(vmem)
        moved += 6 * height * width
        flops += 2 * height * width * own[1][1].shape[0]
    if outer:
        mean, anchor, moment, so_far = outer[1]
        if so_far:
            aliases = {len(operands) + 3: len(outs), len(operands) + 4: len(outs) + 1}
        operands += [mean, *stay([anchor, moment]), *so_far]
        specs += [vmem] + [hbm] * (2 + len(so_far))
        outs += [pltpu.HBM(anchor.shape, BF16)] * 2
        out_specs += [hbm, hbm]
        moved += 8 * height * width
    return pl.pallas_call(
        functools.partial(piece_kernel, own and own[0], outer and outer[0]),
        out_shape=outs,
        in_specs=specs,
        out_specs=out_specs,
        scratch_shapes=[
            pltpu.VMEM((5, height, width), BF16),
            pltpu.VMEM((2, height, width), BF16),
            pltpu.SemaphoreType.DMA((7,)),
        ],
        input_output_aliases=aliases,
        cost_estimate=pl.CostEstimate(flops=flops, bytes_accessed=moved, transcendentals=0),
        compiler_params=pltpu.CompilerParams(vmem_limit_bytes=KERNEL_VMEM),
        name="piece",
    )(*operands)


def on_device(fsdp, tensor, hidden, target, valid, island_tokens, inner_weight, adam_first, adam_second, anchor, outer_momentum):
    rows, cols = inner_weight.shape[1:]
    weight = inner_weight[0]
    block = target.shape[1]
    me = lax.axis_index("tensor")
    rings = [[(i, (i + step) % tensor) for i in range(tensor)] for step in range(1, tensor)]
    width = cols // QUARTERS
    height = rows // ROW_BLOCKS

    def share(tokens, columns):
        return (jnp.dot(tokens, weight[:, columns], preferred_element_type=F32) * SHARE).astype(F16)

    def part(array, owner):
        return lax.dynamic_slice_in_dim(array, owner * block, block, axis=0)

    def hand_out(partial):
        return [
            lax.ppermute(part(partial, lax.rem(me + step, tensor)), "tensor", ring)
            for step, ring in enumerate(rings, 1)
        ]

    def finish(total, columns):
        keep = part(valid_all, me)[:, None]
        output = keep * total * (factor / SHARE)
        wanted = target[0, :, columns].astype(F32)
        return (keep * ((output - wanted) / tallies)).astype(BF16)

    def hand_round(cot):
        return [lax.ppermute(cot, "tensor", ring) for ring in rings]

    def assemble(cot, arrived):
        whole = jnp.zeros((block * tensor, cot.shape[1]), BF16)
        whole = lax.dynamic_update_slice_in_dim(whole, cot, me * block, axis=0)
        for step, piece in enumerate(arrived, 1):
            owner = lax.rem(me + (tensor - step), tensor)
            whole = lax.dynamic_update_slice_in_dim(whole, piece, owner * block, axis=0)
        return whole

    lead, rest = slice(0, width), slice(width, cols)
    valid_own = valid[0].astype(F32)
    if fsdp == 2:
        swap = [(0, 1), (1, 0)]
        leading = lax.axis_index("fsdp") == 0

        def in_order(a, b):
            return jnp.concatenate([jnp.where(leading, a, b), jnp.where(leading, b, a)], axis=0)

        other = lax.ppermute(hidden[0], "fsdp", swap)
        valid_other = lax.ppermute(valid_own, "fsdp", swap)
        near, near_rest = share(hidden[0], lead), share(hidden[0], rest)
        (near, near_rest), own_tokens = fence(((near, near_rest), hidden[0]))
        partial = in_order(near, share(other, lead))
    else:
        tokens = lax.all_gather(hidden[0], "fsdp", axis=0, tiled=True)
        valid_all = lax.all_gather(valid_own, "fsdp", axis=0, tiled=True)
        partial = share(tokens, lead)
    sends = [part(partial, lax.rem(me + step, tensor)) for step in range(1, tensor)]
    if fsdp == 2:
        sends, partial, other = fence((sends, partial, other))
    shares = [lax.ppermute(send, "tensor", ring) for send, ring in zip(sends, rings)]
    if fsdp == 2:
        partial, own_tokens, other, valid_own, valid_other = fence((partial, own_tokens, other, valid_own, valid_other))
        tokens = in_order(own_tokens, other)
        valid_all = in_order(valid_own, valid_other)
    tallies = jnp.sum(valid_all)
    total = part(partial, me).astype(F32)
    for piece in shares:
        total += piece.astype(F32)
    mine = finish(total, lead)
    cot = assemble(mine, hand_round(mine))

    island = lax.axis_index("island")
    at_end = (island == 0) | (island == 3)
    totals = island_tokens.astype(F32)
    portion = (jnp.sum(jnp.where(jnp.arange(4) == island, totals, 0.0)) / jnp.sum(totals)).reshape(1)

    def plus(a, b):
        return (a.astype(F32) + b.astype(F32)).astype(F16)

    pieces = [(q, r) for q in range(QUARTERS) for r in range(ROW_BLOCKS)]
    count = len(pieces)
    own = {}

    def wanted(event, cot):
        q, r = pieces[event]
        at = (r * height, q * width, 0 if q == 0 else (q - 1) * width)
        return at, (portion, tokens, cot, inner_weight, adam_first, adam_second)

    (own[0],) = work((height, width), wanted(0, cot))
    outs = ()
    sent_end, sent_mid, got_end, got_mid = {}, {}, {}, {}
    shares, handed, steps = [], [], tensor - 1
    shares_event, round_event, ready_event = 0, steps, 2 * steps
    for event in range(count + 3 * LAG):
        held = {}
        if event - LAG in got_end:
            held["got_end"] = got_end.pop(event - LAG)
            held["sent_end"] = sent_end.pop(event - LAG)
        if event - LAG in got_mid:
            held["got_mid"] = got_mid.pop(event - LAG)
            held["sent_mid"] = sent_mid.pop(event - LAG)
        if shares_event < event <= round_event:
            held["share"] = shares.pop()
        if round_event < event <= ready_event:
            held["round"] = handed.pop()
        before = {}
        if event - 1 in sent_end:
            before["end"] = sent_end[event - 1]
        if event - 1 in sent_mid:
            before["mid"] = sent_mid[event - 1]
        if event > count + 2 * LAG:
            before["outs"] = outs
        if held:
            held, before = fence((held, before))
            outs = before.get("outs", outs)
            if "end" in before:
                sent_end[event - 1] = before["end"]
            if "mid" in before:
                sent_mid[event - 1] = before["mid"]
        summed = None
        if event - LAG in range(LAG, count + LAG):
            summed = plus(held["sent_mid"], held["got_mid"])
        now = {}
        if event < count:
            mine_now = own[event].astype(F16) if summed is None else jnp.where(at_end, own[event], summed.astype(F32)).astype(F16)
            now["end"] = mine_now
        elif summed is not None:
            now["end"] = summed
        if event - LAG in own:
            now["mid"] = plus(own.pop(event - LAG), held["got_end"])
        later = {}
        k = event - 3 * LAG
        if k >= 0:
            later["ends"] = (held["got_end"], held["sent_end"])
        if event + 1 < count:
            later["cot"] = cot
        if event == shares_event:
            later["rest"] = (near_rest, other) if fsdp == 2 else tokens
        if shares_event < event < round_event:
            later["partial"] = partial
        if round_event < event < ready_event:
            later["mine"] = mine
        if shares_event < event <= round_event:
            later["share"] = held["share"]
        if round_event < event <= ready_event:
            later["round"] = held["round"]
        now, later = fence((now, later))
        cot = later.get("cot", cot)
        if "end" in now:
            sent_end[event] = now["end"]
            got_end[event] = lax.ppermute(now["end"], "island", ENDS)
        if "mid" in now:
            sent_mid[event] = now["mid"]
            got_mid[event] = lax.ppermute(now["mid"], "island", MIDDLE)
        if event == shares_event:
            if fsdp == 2:
                partial = in_order(later["rest"][0], share(later["rest"][1], rest))
            else:
                partial = share(later["rest"], rest)
            total = part(partial, me).astype(F32)
        if shares_event < event <= round_event:
            total = total + later["share"].astype(F32)
        partial, mine = later.get("partial", partial), later.get("mine", mine)
        if shares_event <= event < round_event:
            step = event - shares_event + 1
            shares.append(lax.ppermute(part(partial, lax.rem(me + step, tensor)), "tensor", rings[step - 1]))
        if event == round_event:
            mine = finish(total, rest)
            rounds = []
        if round_event < event <= ready_event:
            rounds.append(later["round"])
        if round_event <= event < ready_event:
            handed.append(lax.ppermute(mine, "tensor", rings[event - round_event]))
        if event == ready_event:
            cot = assemble(mine, rounds)
        own_next = wanted(event + 1, cot) if event + 1 < count else None
        outer_now = None
        if k >= 0:
            q, r = pieces[k]
            mean = jnp.where(at_end, *later["ends"]).astype(F32) * (1.0 / WIRE)
            outer_now = ((r * height, q * width), (mean, anchor, outer_momentum, outs))
        if own_next or outer_now:
            done = work((height, width), own_next, outer_now)
            if own_next:
                own[event + 1] = done[0]
            if outer_now:
                outs = tuple(done[-2:])
    return outs


def solution(mesh):
    return jax.shard_map(
        functools.partial(on_device, mesh.shape["fsdp"], mesh.shape["tensor"]),
        mesh=mesh,
        in_specs=(
            P("island", "fsdp", "tensor"),
            P("island", "tensor", "fsdp"),
            P("island", "fsdp"),
            P(),
            P("island", "tensor", "fsdp"),
            P("island", "tensor", "fsdp"),
            P("island", "tensor", "fsdp"),
            P("tensor", "fsdp"),
            P("tensor", "fsdp"),
        ),
        out_specs=(P("tensor", "fsdp"), P("tensor", "fsdp")),
        check_vma=False,
    )
```
